256 devices in a mesh: seq: 64 (over y, z, core), ch: 4 (over x).
Axes of the slice: x: 4, y: 4, z: 8, core: 2. Of those that a mesh axis runs over, the one named last changes fastest.
Arguments:
- features: bfloat16 [32768, 1024], P('seq', 'ch'), may hold values from -6 to 6
- w_in: bfloat16 [1024, 3, 1024], P(None, None, 'ch'), may hold values from -0.1875 to 0.1875
- bias_skip: float32 [1024], P('ch'), may hold values from -3 to 3
- filters: float32 [32768, 1024], P('seq', 'ch')
- w_out: bfloat16 [1024, 1024], P(None, 'ch'), may hold values from -0.1875 to 0.1875
- w_emb: bfloat16 [1024, 128], P('ch'), may hold values from -0.1875 to 0.1875
- page_lengths: int32 [512], replicated, may hold values from 1 to 256, 32768 in all
- page_owner: int32 [512], replicated, may hold values from 0 to 63
Outputs:
- index_rows: bfloat16 [32768, 128], P('seq')
The draws below stay inside these ranges and needn't reach their ends.
Inputs may be any that keep to these rules, and one draw needn't show every extreme that they name: page_lengths sum to 32768, and the longest page has exactly 256 patches.
All inputs are finite; a program needn't handle non-finite values.
Results may differ from the reference program's by a relative error of at most 0.0057.
Values may be sent and summed in bfloat16 or wider, within the bound.
A program may use at most 64 MiB of HBM per device.

```python
import math
import jax
import jax.numpy as jnp
import numpy as np

D = 1024
EMB = 128
TOKEN_COUNT = 32768
PAGES = 512
MOST = 256
N_SEQ = 64


def draw_filters(key, part):
    key_pick, key_slow, key_fast, key_lag_offsets, key_noise = jax.random.split(key, 5)
    lag_dimension = jnp.arange(TOKEN_COUNT, dtype=jnp.float32)[:, None]
    slow_share = 0.5
    chosen = jax.random.uniform(key_pick, (D,)) < slow_share
    slow_rate = jnp.exp(jax.random.uniform(key_slow, (D,), minval=math.log(0.5 / TOKEN_COUNT), maxval=math.log(2.0 / TOKEN_COUNT)))
    fast_rate = jnp.exp(jax.random.uniform(key_fast, (D,), minval=math.log(1.0 / 48.0), maxval=math.log(1.0 / 24.0)))
    falloff_speed = jnp.where(chosen, slow_rate, fast_rate)
    spike_lag_positions = jax.random.randint(key_lag_offsets, (3,), 1, TOKEN_COUNT)
    lag_survived = jnp.sum((jnp.arange(TOKEN_COUNT, dtype=jnp.int32)[:, None] >= spike_lag_positions[None, :]).astype(jnp.float32), axis=1)
    spike_train = jnp.power(0.6, lag_survived)[:, None]
    decay_profile = jnp.exp(-falloff_speed[None, :] * lag_dimension) * spike_train
    energy = jnp.expm1(-2.0 * falloff_speed * TOKEN_COUNT) / jnp.expm1(-2.0 * falloff_speed)
    noise = jax.random.normal(key_noise, (TOKEN_COUNT, D))
    return (noise * decay_profile / jnp.sqrt(energy)[None, :]).astype(jnp.float32)


def place_ends(result, key, low, largest):
    spot = [jax.random.randint(jax.random.fold_in(key, axis), (), 0, length) for axis, length in enumerate(result.shape)]
    main_axis = result.shape.index(max(result.shape))
    next_to = spot[:main_axis] + [(spot[main_axis] + 1) % result.shape[main_axis]] + spot[main_axis + 1:]
    return result.at[tuple(spot)].set(low).at[tuple(next_to)].set(largest)


def block_scale(rng, extent, shards, smallest, high):
    def one(axis_at, parts):
        heights = jax.random.uniform(jax.random.fold_in(jax.random.fold_in(rng, 6), axis_at), (parts,), jnp.float32, smallest / len(shards), high / len(shards))
        return jnp.repeat(jnp.exp(heights), extent[axis_at] // parts).reshape((-1,) + (1,) * (len(extent) - axis_at - 1))

    loudness = one(*shards[0])
    for cut in shards[1:]:
        loudness = loudness * one(*cut)
    return loudness


def rank_table(amount, lean):
    loads = [(1 << 20) // math.isqrt(grade ** lean) + 1 for grade in range(1, amount + 1)]
    scale = 1 + sum(loads) // (1 << 30)
    return np.cumsum(np.array([max(1, weight // scale) for weight in loads]))


def skewed_ids(key, dims, number_of, lean):
    table = rank_table(number_of, lean)
    ticket = jax.random.randint(jax.random.fold_in(key, 1), dims, 0, int(table[number_of - 1]))
    rank = jnp.searchsorted(jnp.asarray(table, jnp.int32), ticket, side="right")
    return jax.random.permutation(jax.random.fold_in(key, 2), number_of)[rank].astype(jnp.int32)


def split_up(amount, total, reach, lean):
    portions = [(1 << 20) // math.isqrt(grade ** lean) + 1 for grade in range(2, amount + 1)]
    rest, counts = total - reach - (amount - 1), [1] * (amount - 1)
    while rest > 0:
        free = [i for i in range(amount - 1) if counts[i] < reach]
        mass, left = sum([portions[i] for i in free]), rest
        for i in free:
            addition = min(reach - counts[i], max(1, left * portions[i] // mass), rest)
            counts[i] = counts[i] + addition
            rest = rest - addition
    return np.array([reach] + counts)


def ragged_sizes(stream_key, number_of, total, limit, skew):
    if number_of == 2:
        one = jax.random.randint(stream_key, (), max(1, total - limit), min(limit, total - 1) + 1)
        return jnp.stack([one, total - one])
    sizes = jnp.asarray(split_up(number_of, total, limit, skew), jnp.int32)
    pairs = (number_of - 1) // 2
    giver, receiver = sizes[1:1 + 2 * pairs:2], sizes[2:2 + 2 * pairs:2]
    slack = jnp.minimum(giver - 1, limit - receiver)
    shifted = jax.random.randint(jax.random.fold_in(stream_key, 1), (pairs,), 0, 1 << 20) % (slack + 1)
    sizes = sizes.at[1:1 + 2 * pairs:2].set(giver - shifted).at[2:2 + 2 * pairs:2].set(receiver + shifted)
    return sizes[jax.random.permutation(jax.random.fold_in(stream_key, 2), number_of)]


def normal_values(key, extent, width, reach, shards=(), kind=jnp.bfloat16):
    loudness = block_scale(key, extent, shards, -0.22, 0.18) if shards else 1.0
    drawn = jax.random.normal(key, extent, jnp.float32) * width * loudness
    return jnp.minimum(jnp.maximum(drawn, -reach), reach).astype(kind)


def setup_inputs(seed: int = 0) -> dict:
    arg_keys = jax.random.split(jax.random.key(seed), 9)
    return {
        "features": normal_values(arg_keys[0], (TOKEN_COUNT, D), 1.0, 6.0, ((0, 64), (1, 4))),
        "w_in": normal_values(arg_keys[1], (D, 3, D), D ** -0.5, 0.1875, ((2, 4),)),
        "bias_skip": normal_values(arg_keys[2], (D,), 1.0, 3.0, ((0, 4),), jnp.float32),
        "filters": draw_filters(jax.random.fold_in(arg_keys[8], 71), 0),
        "w_out": normal_values(arg_keys[4], (D, D), D ** -0.5, 0.1875, ((1, 4),)),
        "w_emb": normal_values(arg_keys[5], (D, EMB), D ** -0.5, 0.1875, ((0, 4),)),
        "page_lengths": ragged_sizes(arg_keys[6], PAGES, TOKEN_COUNT, MOST, 2).astype(jnp.int32),
        "page_owner": place_ends(skewed_ids(arg_keys[7], (PAGES,), N_SEQ, 2), jax.random.fold_in(arg_keys[7], 3), 0, N_SEQ - 1).astype(jnp.int32),
    }


def reference(features, w_in, bias_skip, filters, w_out, w_emb, page_lengths, page_owner):
    projected = jnp.dot(features, w_in.reshape(D, 3 * D), preferred_element_type=jnp.float32).reshape(TOKEN_COUNT, 3, D)
    gate_branch = projected[:, 0]
    left_branch = projected[:, 1]
    value_branch = projected[:, 2]
    signal = left_branch * value_branch
    fft_length = 2 * TOKEN_COUNT
    spectrum = jnp.fft.rfft(signal, n=fft_length, axis=0) * jnp.fft.rfft(filters, n=fft_length, axis=0)
    convolved = jnp.fft.irfft(spectrum, n=fft_length, axis=0)[:TOKEN_COUNT].astype(signal.dtype)
    mixed = ((convolved + bias_skip[None, :] * signal) * gate_branch).astype(jnp.bfloat16)
    layer_out = (jnp.dot(mixed, w_out, preferred_element_type=jnp.float32) + features.astype(jnp.float32)).astype(jnp.bfloat16)
    embedded = jnp.dot(layer_out, w_emb, preferred_element_type=jnp.float32).astype(jnp.bfloat16)
    token_owner = jnp.repeat(page_owner, page_lengths, total_repeat_length=TOKEN_COUNT).astype(jnp.int32)
    ordering = jnp.argsort(token_owner, stable=True).astype(jnp.int32)
    return embedded[ordering]
```

```python
import functools
import math

import jax
import jax.numpy as jnp
import ml_dtypes
import numpy as np
from jax import lax
from jax.experimental import pallas as pl
from jax.experimental.pallas import tpu as pltpu
from jax.sharding import PartitionSpec as P

MESH = pl.DeviceIdType.MESH
LANES = 128
CORES = 2
OWNED = 4
F32 = jnp.float32
BF16 = jnp.bfloat16


def dot(a, b, contract=((1,), (0,))):
    return lax.dot_general(a, b, (contract, ((), ())), preferred_element_type=F32)


def split(values):
    high = values.astype(BF16)
    return high, (values - high.astype(F32)).astype(BF16)


def split_table(values):
    high = values.astype(ml_dtypes.bfloat16)
    return np.stack([high, (values - high.astype(np.float64)).astype(ml_dtypes.bfloat16)])


def transform_tables(blocks):
    length = blocks * LANES
    shifted = np.arange(blocks, dtype=np.float64) + 0.25
    outer = 2.0 * math.pi * shifted[:, None] * np.arange(blocks)[None, :] / blocks
    first = np.concatenate([np.cos(outer), -np.sin(outer)], axis=0)
    twist = 2.0 * math.pi * shifted[:, None] * np.arange(LANES)[None, :] / length
    lane = np.arange(LANES)
    inner = 2.0 * math.pi * (lane[:, None] * lane[None, :] % LANES) / LANES
    second = np.block([[np.cos(inner), -np.sin(inner)], [np.sin(inner), np.cos(inner)]])
    return (
        split_table(first),
        np.stack([np.cos(twist), np.sin(twist)]).astype(np.float32),
        split_table(second),
        split_table(second.T),
        split_table(first.T / length),
    )


def exact3(data, table, data_left=True):
    high, low = split(data)
    if data_left:
        return dot(high, table[0]) + dot(low, table[0]) + dot(high, table[1])
    return dot(table[0], high) + dot(table[0], low) + dot(table[1], high)


def side_by_side(parts):
    return jnp.concatenate(parts, axis=1)


def forward(values, first, twist, second):
    blocks = values.shape[0]
    stage = dot(first[0], values) + dot(first[1], values)
    real, imag = stage[:blocks], stage[blocks:]
    cos, sin = twist[0], twist[1]
    rows = []
    for c in range(OWNED):
        lanes = slice(c * LANES, (c + 1) * LANES)
        r, i = real[:, lanes], imag[:, lanes]
        rows.append(side_by_side([r * cos + i * sin, i * cos - r * sin]))
    return exact3(jnp.concatenate(rows, axis=0), second)


def multiply(a, b):
    ar, ai, br, bi = a[:, :LANES], a[:, LANES:], b[:, :LANES], b[:, LANES:]
    return side_by_side([ar * br - ai * bi, ar * bi + ai * br])


def backward(spectrum, last, twist, second):
    blocks = spectrum.shape[0] // OWNED
    stage = exact3(spectrum, second)
    cos, sin = twist[0], twist[1]
    real, imag = [], []
    for c in range(OWNED):
        rows = stage[c * blocks : (c + 1) * blocks]
        r, i = rows[:, :LANES], rows[:, LANES:]
        real.append(r * cos - i * sin)
        imag.append(i * cos + r * sin)
    return exact3(
        jnp.concatenate([side_by_side(real), side_by_side(imag)], axis=0), last, data_left=False
    )


def layer_kernel(
    sizes,
    features, w_in, bias, filters, w_out, w_emb, lengths, owners,
    first_t, twist_t, second_t, second_back_t, last_t,
    out,
    feat, w_vm, w_turned, filt_vm, w_out_vm, w_emb_vm, first_v, twist_v, second_v, second_back_v, last_v,
    stage, filt_send, filt_recv, sig_send, sig_recv, conv_send, conv_recv,
    signal_t, gate_t, spectrum, term_send, term_recv, weight_high, weight_low,
    emb_send, emb_recv, table, chosen, contrib, from_core, joined, joined_recv,
    local_sem, feat_send_sem, feat_recv_sem, turn_send_sem, turn_recv_sem,
    term_send_sem, term_recv_sem, emb_send_sem, emb_recv_sem,
    z_send_sem, z_recv_sem, y_send_sem, y_recv_sem, core_sem, join_send_sem, join_recv_sem,
):
    seq_n, ch_n, y_n, z_n = sizes
    rows_dev, chan_dev = filters.shape
    quads = rows_dev // LANES
    pack = quads * OWNED
    blocks = seq_n * quads
    part_rows = rows_dev // ch_n
    me, ch = lax.axis_index("seq"), lax.axis_index("ch")
    core = lax.rem(me, CORES)
    place = lax.div(me, CORES)
    my_z = lax.rem(place, z_n)
    my_y = lax.div(place, z_n)

    def seq_peer(i):
        return lax.rem(me + i, seq_n)

    def ch_peer(i):
        return lax.rem(ch + i, ch_n)

    barrier = pltpu.get_barrier_semaphore()

    @pl.loop(1, seq_n)
    def _(i):
        pl.semaphore_signal(barrier, inc=1, device_id=(seq_peer(i), ch), device_id_type=MESH)

    for i in range(1, ch_n):
        pl.semaphore_signal(barrier, inc=1, device_id=(me, ch_peer(i)), device_id_type=MESH)

    loads = [
        (filters, filt_vm), (w_in, w_vm), (features, feat.at[ch]), (first_t, first_v), (twist_t, twist_v),
        (second_t, second_v), (w_out, w_out_vm), (w_emb, w_emb_vm), (second_back_t, second_back_v), (last_t, last_v),
    ]
    loads = [pltpu.make_async_copy(a, b, local_sem.at[n]) for n, (a, b) in enumerate(loads)]
    for load in loads:
        load.start()

    def scatter(send, recv, n):
        @pl.loop(1, seq_n)
        def _(i):
            peer = seq_peer(i)
            pltpu.make_async_remote_copy(
                src_ref=send.at[pl.ds(pl.multiple_of(peer * pack, pack), pack)],
                dst_ref=recv.at[pl.ds(pl.multiple_of(me * pack, pack), pack)],
                send_sem=turn_send_sem.at[n],
                recv_sem=turn_recv_sem.at[n],
                device_id=(peer, ch),
                device_id_type=MESH,
            ).start()

        mine = pl.ds(pl.multiple_of(me * pack, pack), pack)
        recv[mine] = send[mine]

    def gathered(send, recv, n):
        most = pl.ds(0, (seq_n - 1) * pack)
        whole = pltpu.make_async_remote_copy(
            src_ref=send.at[most], dst_ref=recv.at[most], send_sem=turn_send_sem.at[n],
            recv_sem=turn_recv_sem.at[n], device_id=(seq_peer(1), ch), device_id_type=MESH,
        )
        whole.wait_send()
        whole.wait_recv()

    def chunks_by_channel(turned, send):
        for q in range(quads):
            for c in range(OWNED):
                stage[pl.ds(q * OWNED + c, seq_n, pack), :] = turned[
                    c * seq_n : (c + 1) * seq_n, q * LANES : (q + 1) * LANES
                ]
        send[...] = stage[...].astype(BF16)

    def whole_document(recv):
        stage[...] = recv[...].astype(F32)
        return side_by_side([stage[pl.ds(c, blocks, OWNED), :] for c in range(OWNED)]).astype(BF16)

    loads[0].wait()
    chunks_by_channel(filt_vm[...].T, filt_send)
    loads[1].wait()
    for b in range(3):
        w_turned[b] = w_vm[b].T

    pl.semaphore_wait(barrier, seq_n - 1 + ch_n - 1)
    loads[2].wait()

    def feature_copy(i):
        return pltpu.make_async_remote_copy(
            src_ref=feat.at[ch], dst_ref=feat.at[ch], send_sem=feat_send_sem.at[i], recv_sem=feat_recv_sem.at[i],
            device_id=(me, ch_peer(i)), device_id_type=MESH,
        )

    for i in (1, ch_n - 1, *range(2, ch_n - 1)) if ch_n > 2 else (1,):
        feature_copy(i).start()
    scatter(filt_send, filt_recv, 0)

    loads[6].wait()
    loads[7].wait()
    emb_turned = w_emb_vm[...].astype(F32).T.astype(BF16)
    term = dot(emb_turned, w_out_vm[...], ((1,), (1,)))
    for c in range(ch_n):
        term_send[c] = term[:, c * chan_dev : (c + 1) * chan_dev]

    def add_projection(source, first_time):
        block = feat[source]
        for b in range(3):
            lanes = pl.ds(pl.multiple_of(source * chan_dev, chan_dev), chan_dev)
            product = dot(w_turned[b, :, lanes], block, ((1,), (1,)))
            target = (gate_t, signal_t, spectrum)[b]
            if b == 2:
                view = pl.ds(0, chan_dev)
                for q in range(2):
                    lanes2 = slice(q * 2 * LANES, (q + 1) * 2 * LANES)
                    rows = pl.ds(q * chan_dev, chan_dev)
                    if first_time:
                        spectrum[rows, :] = product[:, lanes2]
                    else:
                        spectrum[rows, :] += product[:, lanes2]
            elif first_time:
                target[...] = product
            else:
                target[...] += product

    add_projection(ch, True)
    for i in (1, ch_n - 1, *range(2, ch_n - 1)) if ch_n > 2 else (1,):
        feature_copy(i).wait_recv()
        add_projection(lax.rem(ch + ch_n - i, ch_n), False)
    value = side_by_side([spectrum[:chan_dev, :], spectrum[chan_dev : 2 * chan_dev, :]])
    signal_t[...] = signal_t[...] * value
    chunks_by_channel(signal_t[...], sig_send)
    scatter(sig_send, sig_recv, 1)

    def term_copy(i):
        return pltpu.make_async_remote_copy(
            src_ref=term_send.at[ch_peer(i)], dst_ref=term_recv.at[ch], send_sem=term_send_sem.at[i],
            recv_sem=term_recv_sem.at[i], device_id=(me, ch_peer(i)), device_id_type=MESH,
        )

    for i in range(1, ch_n):
        term_copy(i).start()
    term_recv[ch] = term_send[ch]

    gathered(filt_send, filt_recv, 0)
    for n in (3, 4, 5):
        loads[n].wait()
    spectrum[...] = forward(whole_document(filt_recv), first_v, twist_v, second_v)

    pages = lengths.shape[1]
    length_row = lengths[...].astype(F32)
    owner_row = owners[...].astype(F32)
    length_col = jnp.broadcast_to(length_row, (LANES, pages)).T
    owner_col = side_by_side([jnp.broadcast_to(owner_row, (LANES, pages)).T] * (pages // LANES))
    here = lax.broadcasted_iota(jnp.int32, (pages, pages), 0)
    other = lax.broadcasted_iota(jnp.int32, (pages, pages), 1)
    earlier = jnp.where(other < here, 1.0, 0.0)
    ahead = jnp.where(owner_row < owner_col, 1.0, jnp.where(owner_row == owner_col, earlier, 0.0))
    length_b = length_col.astype(BF16)
    placed = dot(ahead.astype(BF16), length_b)
    move = dot(earlier.astype(BF16), length_b) - placed
    move_high = jnp.floor(move * (1.0 / 256.0))
    move_low = (move - 256.0 * move_high).astype(BF16)
    placed_row = placed.T[0:1]
    chip_rows = CORES * rows_dev
    row0 = place * chip_rows
    position = (lax.broadcasted_iota(jnp.int32, (chip_rows, pages), 0) + row0).astype(F32)
    inside = jnp.where(position >= placed_row, jnp.where(position < placed_row + length_row, 1.0, 0.0), 0.0)
    inside = inside.astype(BF16)
    source = (
        position[:, :LANES] + 256.0 * dot(inside, move_high.astype(BF16)) + dot(inside, move_low)
    ).astype(jnp.int32)
    in_part = source & (part_rows - 1)
    token_part = (source >> int(math.log2(part_rows))) & (ch_n - 1)
    token_core = (source >> int(math.log2(rows_dev))) & (CORES - 1)
    token_place = source >> int(math.log2(chip_rows))
    slot = jnp.where(token_part == ch, jnp.where(token_core == core, token_place * part_rows + in_part, -1), -1)
    lane = lax.broadcasted_iota(jnp.int32, (chip_rows, LANES), 1)
    for b in range(chosen.shape[1] // LANES):
        chosen[:, b * LANES : (b + 1) * LANES] = jnp.where(slot == lane + b * LANES, 1.0, 0.0).astype(BF16)

    gathered(sig_send, sig_recv, 1)
    product = multiply(forward(whole_document(sig_recv), first_v, twist_v, second_v), spectrum[...])
    for n in (8, 9):
        loads[n].wait()
    convolved = backward(product, last_v, twist_v, second_back_v)
    for c in range(OWNED):
        stage[pl.ds(c, blocks, OWNED), :] = convolved[:, c * LANES : (c + 1) * LANES]
    conv_send[...] = stage[...].astype(BF16)
    scatter(conv_send, conv_recv, 2)

    for i in range(1, ch_n):
        term_copy(i).wait_recv()
    weight = term_recv[0]
    for c in range(1, ch_n):
        weight = weight + term_recv[c]
    weight_high[...], weight_low[...] = split(weight)
    own_part = dot(emb_turned, feat[ch], ((1,), (1,)))
    bias_col = side_by_side([jnp.broadcast_to(bias[...], (LANES, chan_dev)).T] * quads)
    skipped = bias_col * signal_t[...]

    gathered(conv_send, conv_recv, 2)
    stage[...] = conv_recv[...].astype(F32)
    convolved_t = jnp.concatenate(
        [
            side_by_side([stage[pl.ds(q * OWNED + c, seq_n, pack), :] for q in range(quads)])
            for c in range(OWNED)
        ],
        axis=0,
    )
    mixed = ((convolved_t + skipped) * gate_t[...]).astype(BF16)
    embedded = (dot(weight_high[...], mixed) + dot(weight_low[...], mixed) + own_part).T
    for c in range(ch_n):
        emb_send[c] = embedded[c * part_rows : (c + 1) * part_rows]

    def emb_copy(i):
        return pltpu.make_async_remote_copy(
            src_ref=emb_send.at[ch_peer(i)], dst_ref=emb_recv.at[ch], send_sem=emb_send_sem.at[i],
            recv_sem=emb_recv_sem.at[i], device_id=(me, ch_peer(i)), device_id_type=MESH,
        )

    for i in range(1, ch_n):
        emb_copy(i).start()
    emb_recv[ch] = emb_send[ch]
    for i in range(1, ch_n):
        emb_copy(i).wait_recv()
    total = emb_recv[0]
    for c in range(1, ch_n):
        total = total + emb_recv[c]
    table[place] = total.astype(BF16)

    def seq_of(y, z, k):
        return (y * z_n + z) * CORES + k

    def z_copy(i):
        return pltpu.make_async_remote_copy(
            src_ref=table.at[place], dst_ref=table.at[place], send_sem=z_send_sem.at[i], recv_sem=z_recv_sem.at[i],
            device_id=(seq_of(my_y, lax.rem(my_z + i, z_n), core), ch), device_id_type=MESH,
        )

    def y_copy(i, j):
        spot = my_y * z_n + lax.rem(my_z + z_n - j, z_n)
        return pltpu.make_async_remote_copy(
            src_ref=table.at[spot], dst_ref=table.at[spot], send_sem=y_send_sem.at[i, j], recv_sem=y_recv_sem.at[i, j],
            device_id=(seq_of(lax.rem(my_y + i, y_n), my_z, core), ch), device_id_type=MESH,
        )

    order = sorted(range(1, z_n), key=lambda i: min(i, z_n - i))
    for i in order:
        z_copy(i).start()
    for j in [0, *order]:
        if j:
            z_copy(j).wait_recv()
        for i in range(1, y_n):
            y_copy(i, j).start()
    for j in [0, *order]:
        for i in range(1, y_n):
            y_copy(i, j).wait_recv()

    @pl.loop(0, CORES)
    def _(k):
        rows = pl.ds(pl.multiple_of(k * rows_dev, rows_dev), rows_dev)
        stack = table[...].reshape(y_n * z_n * part_rows, LANES)
        contrib[k] = dot(chosen[rows, :], stack).astype(BF16)

    partner = me + 1 - 2 * core
    swap = pltpu.make_async_remote_copy(
        src_ref=contrib.at[1 - core], dst_ref=from_core, send_sem=core_sem.at[0], recv_sem=core_sem.at[1],
        device_id=(partner, ch), device_id_type=MESH,
    )
    swap.start()
    swap.wait_recv()
    joined[...] = contrib[core] + from_core[...]

    def join_copy(i):
        return pltpu.make_async_remote_copy(
            src_ref=joined, dst_ref=joined_recv.at[ch], send_sem=join_send_sem.at[i], recv_sem=join_recv_sem.at[i],
            device_id=(me, ch_peer(i)), device_id_type=MESH,
        )

    for i in range(1, ch_n):
        join_copy(i).start()
    result = joined[...]
    for i in range(1, ch_n):
        join_copy(i).wait_recv()
        result = result + joined_recv[lax.rem(ch + ch_n - i, ch_n)]
    out[...] = result

    swap.wait_send()
    for i in range(1, ch_n):
        feature_copy(i).wait_send()
        term_copy(i).wait_send()
        emb_copy(i).wait_send()
        join_copy(i).wait_send()
    for i in order:
        z_copy(i).wait_send()
    for j in [0, *order]:
        for i in range(1, y_n):
            y_copy(i, j).wait_send()


def body(sizes, features, w_in, bias_skip, filters, w_out, w_emb, page_lengths, page_owner):
    seq_n, ch_n, y_n, z_n = sizes
    rows_dev, chan_dev = features.shape
    width, emb = w_out.shape[0], w_emb.shape[1]
    quads = rows_dev // LANES
    blocks = seq_n * quads
    turn_rows = seq_n * quads * OWNED
    part_rows = rows_dev // ch_n
    places = y_n * z_n
    tables = [jnp.asarray(t) for t in transform_tables(blocks)]
    vmem, sem = pltpu.VMEM, pltpu.SemaphoreType.DMA
    turn = vmem((turn_rows, LANES), BF16)
    scratch = [
        vmem((ch_n, rows_dev, chan_dev), BF16),
        vmem((3, width, chan_dev), BF16),
        vmem((3, chan_dev, width), BF16),
        vmem((rows_dev, chan_dev), F32),
        vmem(w_out.shape, BF16),
        vmem(w_emb.shape, BF16),
        *(vmem(t.shape, t.dtype) for t in tables),
        vmem((turn_rows, LANES), F32),
        *([turn] * 6),
        vmem((chan_dev, rows_dev), F32),
        vmem((chan_dev, rows_dev), F32),
        vmem((OWNED * blocks, 2 * LANES), F32),
        vmem((ch_n, emb, chan_dev), F32),
        vmem((ch_n, emb, chan_dev), F32),
        vmem((emb, chan_dev), BF16),
        vmem((emb, chan_dev), BF16),
        vmem((ch_n, part_rows, emb), F32),
        vmem((ch_n, part_rows, emb), F32),
        vmem((places, part_rows, emb), BF16),
        vmem((CORES * rows_dev, places * part_rows), BF16),
        vmem((CORES, rows_dev, emb), BF16),
        vmem((rows_dev, emb), BF16),
        vmem((rows_dev, emb), BF16),
        vmem((ch_n, rows_dev, emb), BF16),
        sem((10,)),
        sem((ch_n,)), sem((ch_n,)),
        sem((3,)), sem((3,)),
        sem((ch_n,)), sem((ch_n,)),
        sem((ch_n,)), sem((ch_n,)),
        sem((z_n,)), sem((z_n,)),
        sem((y_n, z_n)), sem((y_n, z_n)),
        sem((2,)),
        sem((ch_n,)), sem((ch_n,)),
    ]
    anywhere = pl.BlockSpec(memory_space=pl.ANY)
    inside = pl.BlockSpec(memory_space=pltpu.VMEM)
    return pl.pallas_call(
        functools.partial(layer_kernel, sizes),
        out_shape=jax.ShapeDtypeStruct((rows_dev, emb), BF16),
        in_specs=[anywhere, anywhere, inside, anywhere, anywhere, anywhere, inside, inside] + [anywhere] * 5,
        out_specs=inside,
        scratch_shapes=scratch,
        compiler_params=pltpu.CompilerParams(
            collective_id=0, has_side_effects=True, vmem_limit_bytes=60 * 1024 * 1024
        ),
        name="hyena_layer",
    )(
        features,
        jnp.transpose(w_in, (1, 0, 2)),
        bias_skip[None, :],
        filters,
        w_out,
        w_emb,
        page_lengths[None, :],
        page_owner[None, :],
        *tables,
    )


def solution(mesh):
    seq_n, ch_n = mesh.shape["seq"], mesh.shape["ch"]
    places = seq_n // CORES
    z_n = min(8, max(1, places // 2))
    sizes = (seq_n, ch_n, places // z_n, z_n)
    return jax.shard_map(
        functools.partial(body, sizes),
        mesh=mesh,
        in_specs=(
            P("seq", "ch"),
            P(None, None, "ch"),
            P("ch"),
            P("seq", "ch"),
            P(None, "ch"),
            P("ch", None),
            P(),
            P(),
        ),
        out_specs=P("seq", None),
        check_vma=False,
    )
```

```python
import functools
import math

import jax
import jax.numpy as jnp
import ml_dtypes
import numpy as np
from jax import lax
from jax.experimental import pallas as pl
from jax.experimental.pallas import tpu as pltpu
from jax.sharding import PartitionSpec as P

MESH = pl.DeviceIdType.MESH
RING = ("right_low", "right_high", "left_high", "left_low", "right_on", "left_on")
LANES = 128
CORES = 2
OWNED = 4
F32 = jnp.float32
BF16 = jnp.bfloat16


def dot(a, b, contract=((1,), (0,))):
    return lax.dot_general(a, b, (contract, ((), ())), preferred_element_type=F32)


def split(values):
    high = values.astype(BF16)
    return high, (values - high.astype(F32)).astype(BF16)


def split_table(values):
    high = values.astype(ml_dtypes.bfloat16)
    return np.stack([high, (values - high.astype(np.float64)).astype(ml_dtypes.bfloat16)])


def transform_tables(blocks):
    length = blocks * LANES
    shifted = np.arange(blocks, dtype=np.float64) + 0.25
    outer = 2.0 * math.pi * shifted[:, None] * np.arange(blocks)[None, :] / blocks
    first = np.concatenate([np.cos(outer), -np.sin(outer)], axis=0)
    twist = 2.0 * math.pi * shifted[:, None] * np.arange(LANES)[None, :] / length
    lane = np.arange(LANES)
    inner = 2.0 * math.pi * (lane[:, None] * lane[None, :] % LANES) / LANES
    second = np.block([[np.cos(inner), -np.sin(inner)], [np.sin(inner), np.cos(inner)]])
    return (
        split_table(first),
        np.stack([np.cos(twist), np.sin(twist)]).astype(np.float32),
        split_table(second),
        split_table(second.T),
        split_table(first.T / length),
    )


def exact3(data, table, data_left=True):
    high, low = split(data)
    if data_left:
        return dot(high, table[0]) + dot(low, table[0]) + dot(high, table[1])
    return dot(table[0], high) + dot(table[0], low) + dot(table[1], high)


def side_by_side(parts):
    return jnp.concatenate(parts, axis=1)


def forward(values, first, twist, second):
    blocks = values.shape[0]
    stage = dot(first[0], values) + dot(first[1], values)
    real, imag = stage[:blocks], stage[blocks:]
    cos, sin = twist[0], twist[1]
    rows = []
    for c in range(OWNED):
        lanes = slice(c * LANES, (c + 1) * LANES)
        r, i = real[:, lanes], imag[:, lanes]
        rows.append(side_by_side([r * cos + i * sin, i * cos - r * sin]))
    return exact3(jnp.concatenate(rows, axis=0), second)


def multiply(a, b):
    ar, ai, br, bi = a[:, :LANES], a[:, LANES:], b[:, :LANES], b[:, LANES:]
    return side_by_side([ar * br - ai * bi, ar * bi + ai * br])


def backward(spectrum, last, twist, second):
    blocks = spectrum.shape[0] // OWNED
    stage = exact3(spectrum, second)
    cos, sin = twist[0], twist[1]
    real, imag = [], []
    for c in range(OWNED):
        rows = stage[c * blocks : (c + 1) * blocks]
        r, i = rows[:, :LANES], rows[:, LANES:]
        real.append(r * cos - i * sin)
        imag.append(i * cos + r * sin)
    return exact3(
        jnp.concatenate([side_by_side(real), side_by_side(imag)], axis=0), last, data_left=False
    )


def layer_kernel(
    sizes,
    features, w_in, bias, filters, w_out, w_emb, lengths, owners,
    first_t, twist_t, second_t, second_back_t, last_t,
    out,
    feat, w_vm, w_turned, filt_vm, w_out_vm, w_emb_vm, first_v, twist_v, second_v, second_back_v, last_v,
    stage, filt_send, filt_recv, sig_send, sig_recv, conv_send, conv_recv,
    signal_t, gate_t, spectrum, term_send, term_recv, weight_high, weight_low,
    emb_send, emb_recv, map_send, map_recv, chosen, col_send, col_recv, out_send, out_recv, joined,
    local_sem, feat_send_sem, feat_recv_sem, turn_send_sem, turn_recv_sem,
    term_send_sem, term_recv_sem, emb_send_sem, emb_recv_sem,
    join_send_sem, join_recv_sem,
):
    seq_n, ch_n = sizes
    rows_dev, chan_dev = filters.shape
    quads = rows_dev // LANES
    pack = quads * OWNED
    blocks = seq_n * quads
    places = seq_n // CORES
    share = w_emb.shape[1] // ch_n
    me, ch = lax.axis_index("seq"), lax.axis_index("ch")
    core = lax.rem(me, CORES)
    place = lax.div(me, CORES)

    def seq_peer(i):
        return lax.rem(me + i, seq_n)

    def ch_peer(i):
        return lax.rem(ch + i, ch_n)

    sent = []

    def go(copy):
        copy.start()
        sent.append(copy)

    barrier = pltpu.get_barrier_semaphore()

    @pl.loop(1, seq_n)
    def _(i):
        pl.semaphore_signal(barrier, inc=1, device_id=(seq_peer(i), ch), device_id_type=MESH)

    for i in range(1, ch_n):
        pl.semaphore_signal(barrier, inc=1, device_id=(me, ch_peer(i)), device_id_type=MESH)

    loads = [
        (filters, filt_vm), (w_in, w_vm), (features, feat.at[ch]), (first_t, first_v), (twist_t, twist_v),
        (second_t, second_v), (w_out, w_out_vm), (w_emb, w_emb_vm), (second_back_t, second_back_v), (last_t, last_v),
    ]
    loads = [pltpu.make_async_copy(a, b, local_sem.at[n]) for n, (a, b) in enumerate(loads)]
    for load in loads:
        load.start()

    def scatter(send, recv, n):
        @pl.loop(1, seq_n)
        def _(i):
            peer = seq_peer(i)
            pltpu.make_async_remote_copy(
                src_ref=send.at[pl.ds(pl.multiple_of(peer * pack, pack), pack)],
                dst_ref=recv.at[pl.ds(pl.multiple_of(me * pack, pack), pack)],
                send_sem=turn_send_sem.at[n],
                recv_sem=turn_recv_sem.at[n],
                device_id=(peer, ch),
                device_id_type=MESH,
            ).start()

        mine = pl.ds(pl.multiple_of(me * pack, pack), pack)
        recv[mine] = send[mine]

    def same_core(src_of, dst_of, n):
        @pl.loop(1, places)
        def _(i):
            peer = lax.rem(place + i, places)
            pltpu.make_async_remote_copy(
                src_ref=src_of(peer), dst_ref=dst_of(), send_sem=turn_send_sem.at[n], recv_sem=turn_recv_sem.at[n],
                device_id=(peer * CORES + core, ch), device_id_type=MESH,
            ).start()

    def all_in(recv, copies, n):
        most = recv.at[pl.ds(0, copies)]
        whole = pltpu.make_async_remote_copy(
            src_ref=most, dst_ref=most, send_sem=turn_send_sem.at[n],
            recv_sem=turn_recv_sem.at[n], device_id=(seq_peer(1), ch), device_id_type=MESH,
        )
        whole.wait_recv()
        sent.append(whole)

    def gathered(send, recv, n):
        most = pl.ds(0, (seq_n - 1) * pack)
        whole = pltpu.make_async_remote_copy(
            src_ref=send.at[most], dst_ref=recv.at[most], send_sem=turn_send_sem.at[n],
            recv_sem=turn_recv_sem.at[n], device_id=(seq_peer(1), ch), device_id_type=MESH,
        )
        whole.wait_recv()
        sent.append(whole)

    def chunks_by_channel(turned, send):
        for q in range(quads):
            for c in range(OWNED):
                stage[pl.ds(q * OWNED + c, seq_n, pack), :] = turned[
                    c * seq_n : (c + 1) * seq_n, q * LANES : (q + 1) * LANES
                ]
        send[...] = stage[...].astype(BF16)

    def whole_document(recv):
        stage[...] = recv[...].astype(F32)
        return side_by_side([stage[pl.ds(c, blocks, OWNED), :] for c in range(OWNED)]).astype(BF16)

    pages = lengths.shape[1]
    length_row = lengths[...].astype(F32)
    owner_row = owners[...].astype(F32)
    length_col = jnp.broadcast_to(length_row, (LANES, pages)).T
    owner_col = side_by_side([jnp.broadcast_to(owner_row, (LANES, pages)).T] * (pages // LANES))
    here = lax.broadcasted_iota(jnp.int32, (pages, pages), 0)
    other = lax.broadcasted_iota(jnp.int32, (pages, pages), 1)
    earlier = jnp.where(other < here, 1.0, 0.0)
    ahead = jnp.where(owner_row < owner_col, 1.0, jnp.where(owner_row == owner_col, earlier, 0.0))
    length_b = length_col.astype(BF16)
    placed = dot(ahead.astype(BF16), length_b)
    move = dot(earlier.astype(BF16), length_b) - placed
    move_high = jnp.floor(move * (1.0 / 256.0))
    move_low = move - 256.0 * move_high
    begin = side_by_side([placed] * quads)
    end = side_by_side([placed + length_col] * quads)
    position = (lax.broadcasted_iota(jnp.int32, (pages, rows_dev), 1) + me * rows_dev).astype(F32)
    inside = jnp.where(position >= begin, jnp.where(position < end, 1.0, 0.0), 0.0).astype(BF16)
    source = (
        position[:16]
        + 256.0 * dot(move_high.T[:16].astype(BF16), inside)
        + dot(move_low.T[:16].astype(BF16), inside)
    )
    source_block = jnp.floor(source * (1.0 / LANES))
    source_lane = source - LANES * source_block
    for q in range(quads):
        lanes = slice(q * LANES, (q + 1) * LANES)
        map_send[q : q + 1, :] = source_block[:1, lanes]
        map_send[quads + q : quads + q + 1, :] = source_lane[:1, lanes]

    loads[0].wait()
    chunks_by_channel(filt_vm[...].T, filt_send)
    loads[1].wait()
    for b in range(3):
        w_turned[b] = w_vm[b].T

    pl.semaphore_wait(barrier, seq_n - 1 + ch_n - 1)
    loads[2].wait()

    def ring_copy(held, left, right, sems, rows, kind):
        (lane_of, send_sem, recv_sem) = sems
        half = rows // 2
        own, spot, top, device = {
            "right_low": (1, 1, 0, right), "right_high": (1, 1, 1, right),
            "left_high": (1, 1, 1, left), "left_low": (1, 1, 0, left),
            "right_on": (0, 0, 0, right), "left_on": (0, 2, 1, left),
        }[kind]
        block = held(spot).at[pl.ds(top * half, half)]
        n = RING.index(kind)
        return pltpu.make_async_remote_copy(
            src_ref=block, dst_ref=block, send_sem=send_sem.at[(*lane_of, n)], recv_sem=recv_sem.at[(*lane_of, n)],
            device_id=device, device_id_type=MESH,
        )

    def feature_copy(kind):
        return ring_copy(
            lambda spot: feat.at[lax.rem(ch + ch_n - 1 + spot, ch_n)], (me, ch_peer(ch_n - 1)), (me, ch_peer(1)),
            ((), feat_send_sem, feat_recv_sem), rows_dev, kind,
        )

    ring_first = RING[:4] if ch_n == 4 else RING[:2]
    for kind in ring_first:
        go(feature_copy(kind))

    scatter(filt_send, filt_recv, 0)
    map_recv[place] = map_send[...]
    same_core(lambda peer: map_send, lambda: map_recv.at[place], 3)
    if ch_n == 4:
        feature_copy("right_low").wait_recv()
        go(feature_copy("right_on"))
        feature_copy("left_high").wait_recv()
        go(feature_copy("left_on"))
    loads[6].wait()
    loads[7].wait()
    emb_turned = w_emb_vm[...].astype(F32).T.astype(BF16)
    term = dot(emb_turned, w_out_vm[...], ((1,), (1,)))
    for c in range(ch_n):
        term_send[c] = term[:, c * chan_dev : (c + 1) * chan_dev]

    def add_projection(source, first_time):
        block = feat[source]
        for b in range(3):
            lanes = pl.ds(pl.multiple_of(source * chan_dev, chan_dev), chan_dev)
            product = dot(w_turned[b, :, lanes], block, ((1,), (1,)))
            target = (gate_t, signal_t, spectrum)[b]
            if b == 2:
                view = pl.ds(0, chan_dev)
                for q in range(2):
                    lanes2 = slice(q * 2 * LANES, (q + 1) * 2 * LANES)
                    rows = pl.ds(q * chan_dev, chan_dev)
                    if first_time:
                        spectrum[rows, :] = product[:, lanes2]
                    else:
                        spectrum[rows, :] += product[:, lanes2]
            elif first_time:
                target[...] = product
            else:
                target[...] += product

    add_projection(ch, True)
    if ch_n == 4:
        feature_copy("right_high").wait_recv()
        add_projection(ch_peer(3), False)
        feature_copy("left_low").wait_recv()
        add_projection(ch_peer(1), False)
        feature_copy("right_on").wait_recv()
        feature_copy("left_on").wait_recv()
        add_projection(ch_peer(2), False)
    elif ch_n == 2:
        for kind in ring_first:
            feature_copy(kind).wait_recv()
        add_projection(ch_peer(1), False)
    value = side_by_side([spectrum[:chan_dev, :], spectrum[chan_dev : 2 * chan_dev, :]])
    signal_t[...] = signal_t[...] * value
    chunks_by_channel(signal_t[...], sig_send)
    scatter(sig_send, sig_recv, 1)

    def term_copy(i):
        return pltpu.make_async_remote_copy(
            src_ref=term_send.at[ch_peer(i)], dst_ref=term_recv.at[ch], send_sem=term_send_sem.at[i],
            recv_sem=term_recv_sem.at[i], device_id=(me, ch_peer(i)), device_id_type=MESH,
        )

    for i in range(1, ch_n):
        go(term_copy(i))
    term_recv[ch] = term_send[ch]

    gathered(filt_send, filt_recv, 0)
    for n in (3, 4, 5):
        loads[n].wait()
    spectrum[...] = forward(whole_document(filt_recv), first_v, twist_v, second_v)

    gathered(sig_send, sig_recv, 1)
    product = multiply(forward(whole_document(sig_recv), first_v, twist_v, second_v), spectrum[...])
    for n in (8, 9):
        loads[n].wait()
    convolved = backward(product, last_v, twist_v, second_back_v)
    for c in range(OWNED):
        stage[pl.ds(c, blocks, OWNED), :] = convolved[:, c * LANES : (c + 1) * LANES]
    conv_send[...] = stage[...].astype(BF16)
    scatter(conv_send, conv_recv, 2)

    for i in range(1, ch_n):
        term_copy(i).wait_recv()
    weight = term_recv[0]
    for c in range(1, ch_n):
        weight = weight + term_recv[c]
    weight_high[...], weight_low[...] = split(weight)
    all_in(map_recv, places - 1, 3)
    block_row = lax.broadcasted_iota(jnp.int32, (blocks, rows_dev), 0).astype(F32)

    @pl.loop(0, places)
    def _(d):
        row = side_by_side([map_recv[d, q : q + 1, :] for q in range(quads)])
        chosen[d] = jnp.where(block_row == row, 1.0, 0.0).astype(BF16)

    own_part = dot(emb_turned, feat[ch], ((1,), (1,)))
    bias_col = side_by_side([jnp.broadcast_to(bias[...], (LANES, chan_dev)).T] * quads)
    skipped = bias_col * signal_t[...]

    gathered(conv_send, conv_recv, 2)
    stage[...] = conv_recv[...].astype(F32)
    convolved_t = jnp.concatenate(
        [
            side_by_side([stage[pl.ds(q * OWNED + c, seq_n, pack), :] for q in range(quads)])
            for c in range(OWNED)
        ],
        axis=0,
    )
    mixed = ((convolved_t + skipped) * gate_t[...]).astype(BF16)
    embedded = (dot(weight_high[...], mixed) + dot(weight_low[...], mixed) + own_part)
    for c in range(ch_n):
        emb_send[c] = embedded[c * share : (c + 1) * share]

    def emb_copy(i):
        return pltpu.make_async_remote_copy(
            src_ref=emb_send.at[ch_peer(i)], dst_ref=emb_recv.at[ch], send_sem=emb_send_sem.at[i],
            recv_sem=emb_recv_sem.at[i], device_id=(me, ch_peer(i)), device_id_type=MESH,
        )

    for i in range(1, ch_n):
        go(emb_copy(i))
    emb_recv[ch] = emb_send[ch]
    for i in range(1, ch_n):
        emb_copy(i).wait_recv()
    total = emb_recv[0]
    for c in range(1, ch_n):
        total = total + emb_recv[c]
    def spread(rows, target):
        for q in range(quads):
            stage[pl.ds(q, places, quads), :] = rows[:, q * LANES : (q + 1) * LANES]
        target[...] = stage[: places * quads, :].astype(BF16).reshape(places, quads, LANES)

    spread(total, col_send)

    @pl.loop(1, seq_n)
    def _(i):
        peer = seq_peer(i)
        pltpu.make_async_remote_copy(
            src_ref=col_send.at[lax.div(peer, CORES)], dst_ref=col_recv.at[me], send_sem=turn_send_sem.at[4],
            recv_sem=turn_recv_sem.at[4], device_id=(peer, ch), device_id_type=MESH,
        ).start()

    col_recv[me] = col_send[place]
    all_in(col_recv, seq_n - 1, 4)
    column_t = col_recv[...].reshape(blocks, LANES).astype(F32).T.astype(BF16)
    lane_row = lax.broadcasted_iota(jnp.int32, (LANES, rows_dev), 0).astype(F32)

    @pl.loop(0, places)
    def _(d):
        found = dot(column_t, chosen[d])
        row = side_by_side([map_recv[d, quads + q : quads + q + 1, :] for q in range(quads)])
        picked = jnp.sum(jnp.where(lane_row == row, found, 0.0), axis=0, keepdims=True)
        for q in range(quads):
            stage[pl.ds(d * quads + q, 1), :] = picked[:, q * LANES : (q + 1) * LANES]

    out_send[...] = stage[: places * quads, :].astype(BF16).reshape(places, quads, LANES)
    out_recv[place] = out_send[place]
    same_core(lambda peer: out_send.at[peer], lambda: out_recv.at[place], 5)
    all_in(out_recv, places - 1, 5)
    stage[: places * quads, :] = out_recv[...].reshape(places * quads, LANES).astype(F32)
    ordered = side_by_side([stage[pl.ds(q, places, quads), :] for q in range(quads)])
    joined[ch] = ordered.astype(BF16)

    def join_copy(i):
        return pltpu.make_async_remote_copy(
            src_ref=joined.at[ch], dst_ref=joined.at[ch], send_sem=join_send_sem.at[i], recv_sem=join_recv_sem.at[i],
            device_id=(me, ch_peer(i)), device_id_type=MESH,
        )

    for i in range(1, ch_n):
        go(join_copy(i))
    for i in range(1, ch_n):
        join_copy(i).wait_recv()
    out[...] = jnp.concatenate([joined[c].astype(F32) for c in range(ch_n)], axis=0).T.astype(BF16)

    for copy in sent:
        copy.wait_send()


def body(sizes, features, w_in, bias_skip, filters, w_out, w_emb, page_lengths, page_owner):
    seq_n, ch_n = sizes
    rows_dev, chan_dev = features.shape
    width, emb = w_out.shape[0], w_emb.shape[1]
    quads = rows_dev // LANES
    blocks = seq_n * quads
    turn_rows = seq_n * quads * OWNED
    places = seq_n // CORES
    share = emb // ch_n
    tables = [jnp.asarray(t) for t in transform_tables(blocks)]
    vmem, sem = pltpu.VMEM, pltpu.SemaphoreType.DMA
    turn = vmem((turn_rows, LANES), BF16)
    scratch = [
        vmem((ch_n, rows_dev, chan_dev), BF16),
        vmem((3, width, chan_dev), BF16),
        vmem((3, chan_dev, width), BF16),
        vmem((rows_dev, chan_dev), F32),
        vmem(w_out.shape, BF16),
        vmem(w_emb.shape, BF16),
        *(vmem(t.shape, t.dtype) for t in tables),
        vmem((turn_rows, LANES), F32),
        *([turn] * 6),
        vmem((chan_dev, rows_dev), F32),
        vmem((chan_dev, rows_dev), F32),
        vmem((OWNED * blocks, 2 * LANES), F32),
        vmem((ch_n, emb, chan_dev), F32),
        vmem((ch_n, emb, chan_dev), F32),
        vmem((emb, chan_dev), BF16),
        vmem((emb, chan_dev), BF16),
        vmem((ch_n, share, rows_dev), F32),
        vmem((ch_n, share, rows_dev), F32),
        vmem((2 * quads, LANES), F32),
        vmem((places, 2 * quads, LANES), F32),
        vmem((places, blocks, rows_dev), BF16),
        vmem((places, quads, LANES), BF16),
        vmem((seq_n, quads, LANES), BF16),
        vmem((places, quads, LANES), BF16),
        vmem((places, quads, LANES), BF16),
        vmem((ch_n, share, rows_dev), BF16),
        sem((10,)),
        sem((6,)), sem((6,)),
        sem((6,)), sem((6,)),
        sem((ch_n,)), sem((ch_n,)),
        sem((ch_n,)), sem((ch_n,)),
        sem((ch_n,)), sem((ch_n,)),
    ]
    anywhere = pl.BlockSpec(memory_space=pl.ANY)
    inside = pl.BlockSpec(memory_space=pltpu.VMEM)
    return pl.pallas_call(
        functools.partial(layer_kernel, sizes),
        out_shape=jax.ShapeDtypeStruct((rows_dev, emb), BF16),
        in_specs=[anywhere, anywhere, inside, anywhere, anywhere, anywhere, inside, inside] + [anywhere] * 5,
        out_specs=inside,
        scratch_shapes=scratch,
        compiler_params=pltpu.CompilerParams(
            collective_id=0, has_side_effects=True, vmem_limit_bytes=60 * 1024 * 1024
        ),
        name="hyena_layer",
    )(
        features,
        jnp.transpose(w_in, (1, 0, 2)),
        bias_skip[None, :],
        filters,
        w_out,
        w_emb,
        page_lengths[None, :],
        page_owner[None, :],
        *tables,
    )


def solution(mesh):
    sizes = (mesh.shape["seq"], mesh.shape["ch"])
    return jax.shard_map(
        functools.partial(body, sizes),
        mesh=mesh,
        in_specs=(
            P("seq", "ch"),
            P(None, None, "ch"),
            P("ch"),
            P("seq", "ch"),
            P(None, "ch"),
            P("ch", None),
            P(),
            P(),
        ),
        out_specs=P("seq", None),
        check_vma=False,
    )
```

```python
import functools
import math

import jax
import jax.numpy as jnp
import ml_dtypes
import numpy as np
from jax import lax
from jax.experimental import pallas as pl
from jax.experimental.pallas import tpu as pltpu
from jax.sharding import PartitionSpec as P

MESH = pl.DeviceIdType.MESH
RING = ("right_low", "right_high", "left_high", "left_low", "right_on", "left_on")
LANES = 128
CORES = 2
OWNED = 4
F32 = jnp.float32
BF16 = jnp.bfloat16


def dot(a, b, contract=((1,), (0,))):
    return lax.dot_general(a, b, (contract, ((), ())), preferred_element_type=F32)


def split(values):
    high = values.astype(BF16)
    return high, (values - high.astype(F32)).astype(BF16)


def split_table(values):
    high = values.astype(ml_dtypes.bfloat16)
    return np.stack([high, (values - high.astype(np.float64)).astype(ml_dtypes.bfloat16)])


def transform_tables(blocks):
    length = blocks * LANES
    shifted = np.arange(blocks, dtype=np.float64) + 0.25
    outer = 2.0 * math.pi * shifted[:, None] * np.arange(blocks)[None, :] / blocks
    first = np.concatenate([np.cos(outer), -np.sin(outer)], axis=0)
    twist = 2.0 * math.pi * shifted[:, None] * np.arange(LANES)[None, :] / length
    lane = np.arange(LANES)
    inner = 2.0 * math.pi * (lane[:, None] * lane[None, :] % LANES) / LANES
    second = np.block([[np.cos(inner), -np.sin(inner)], [np.sin(inner), np.cos(inner)]])
    return (
        split_table(first),
        np.stack([np.cos(twist), np.sin(twist)]).astype(np.float32),
        split_table(second),
        split_table(second.T),
        split_table(first.T / length),
    )


def exact3(data, table, data_left=True):
    high, low = split(data)
    if data_left:
        return dot(high, table[0]) + dot(low, table[0]) + dot(high, table[1])
    return dot(table[0], high) + dot(table[0], low) + dot(table[1], high)


def side_by_side(parts):
    return jnp.concatenate(parts, axis=1)


def forward(values, first, twist, second):
    blocks = values.shape[0]
    stage = dot(first[0], values) + dot(first[1], values)
    real, imag = stage[:blocks], stage[blocks:]
    cos, sin = twist[0], twist[1]
    rows = []
    for c in range(OWNED):
        lanes = slice(c * LANES, (c + 1) * LANES)
        r, i = real[:, lanes], imag[:, lanes]
        rows.append(side_by_side([r * cos + i * sin, i * cos - r * sin]))
    return exact3(jnp.concatenate(rows, axis=0), second)


def multiply(a, b):
    ar, ai, br, bi = a[:, :LANES], a[:, LANES:], b[:, :LANES], b[:, LANES:]
    return side_by_side([ar * br - ai * bi, ar * bi + ai * br])


def backward(spectrum, last, twist, second):
    blocks = spectrum.shape[0] // OWNED
    stage = exact3(spectrum, second)
    cos, sin = twist[0], twist[1]
    real, imag = [], []
    for c in range(OWNED):
        rows = stage[c * blocks : (c + 1) * blocks]
        r, i = rows[:, :LANES], rows[:, LANES:]
        real.append(r * cos - i * sin)
        imag.append(i * cos + r * sin)
    return exact3(
        jnp.concatenate([side_by_side(real), side_by_side(imag)], axis=0), last, data_left=False
    )


def layer_kernel(
    sizes,
    features, w_in, bias, filters, w_out, w_emb, lengths, owners,
    first_t, twist_t, second_t, second_back_t, last_t,
    out,
    feat, w_vm, w_turned, filt_vm, w_out_vm, w_emb_vm, first_v, twist_v, second_v, second_back_v, last_v,
    stage, filt_send, filt_recv, sig_send, sig_recv, conv_send, conv_recv,
    signal_t, gate_t, spectrum, term_send, term_recv, weight_high, weight_low,
    emb_send, emb_recv, map_send, map_recv, chosen, col_send, col_recv, out_send, out_recv,
    local_sem, feat_send_sem, feat_recv_sem, turn_send_sem, turn_recv_sem,
    term_send_sem, term_recv_sem, emb_send_sem, emb_recv_sem,
    heard_sem,
):
    seq_n, ch_n, y_n, z_n = sizes
    rows_dev, chan_dev = filters.shape
    quads = rows_dev // LANES
    pack = quads * OWNED
    blocks = seq_n * quads
    places = seq_n // CORES
    share = w_emb.shape[1] // ch_n
    me, ch = lax.axis_index("seq"), lax.axis_index("ch")
    core = lax.rem(me, CORES)
    place = lax.div(me, CORES)
    my_y, my_z = lax.div(place, z_n), lax.rem(place, z_n)

    def seq_peer(i):
        return lax.rem(me + i, seq_n)

    def ch_peer(i):
        return lax.rem(ch + i, ch_n)

    sent = []

    def go(copy):
        copy.start()
        sent.append(copy)

    barrier = pltpu.get_barrier_semaphore()

    def seq_of(y, z):
        return (lax.rem(my_y + y, y_n) * z_n + lax.rem(my_z + z, z_n)) * CORES + core

    partner = me + 1 - 2 * core
    z_near = sorted({o % z_n for o in (1, 2, -1, -2)} - {0})
    greeted = [(me, ch_peer(i)) for i in range(1, ch_n)] + [(partner, ch)]
    greeted += [(seq_of(y, 0), ch) for y in range(1, y_n)] + [(seq_of(0, z), ch) for z in z_near]
    for device in greeted:
        pl.semaphore_signal(barrier, inc=1, device_id=device, device_id_type=MESH)

    def tell(n, devices):
        for device in devices:
            pl.semaphore_signal(heard_sem.at[n], inc=1, device_id=device, device_id_type=MESH)

    loads = [
        (filters, filt_vm), (w_in, w_vm), (features, feat.at[ch]), (first_t, first_v), (twist_t, twist_v),
        (second_t, second_v), (w_out, w_out_vm), (w_emb, w_emb_vm), (second_back_t, second_back_v), (last_t, last_v),
    ]
    loads = [pltpu.make_async_copy(a, b, local_sem.at[n]) for n, (a, b) in enumerate(loads)]
    for load in loads:
        load.start()

    def scatter(send, recv, n):
        @pl.loop(1, seq_n)
        def _(i):
            peer = seq_peer(i)
            pltpu.make_async_remote_copy(
                src_ref=send.at[pl.ds(pl.multiple_of(peer * pack, pack), pack)],
                dst_ref=recv.at[pl.ds(pl.multiple_of(me * pack, pack), pack)],
                send_sem=turn_send_sem.at[n],
                recv_sem=turn_recv_sem.at[n],
                device_id=(peer, ch),
                device_id_type=MESH,
            ).start()

        mine = pl.ds(pl.multiple_of(me * pack, pack), pack)
        recv[mine] = send[mine]

    def same_core(src_of, dst_of, n):
        @pl.loop(1, places)
        def _(i):
            peer = lax.rem(place + i, places)
            pltpu.make_async_remote_copy(
                src_ref=src_of(peer), dst_ref=dst_of(), send_sem=turn_send_sem.at[n], recv_sem=turn_recv_sem.at[n],
                device_id=(peer * CORES + core, ch), device_id_type=MESH,
            ).start()

    def all_in(recv, copies, n):
        most = recv.at[pl.ds(0, copies)]
        whole = pltpu.make_async_remote_copy(
            src_ref=most, dst_ref=most, send_sem=turn_send_sem.at[n],
            recv_sem=turn_recv_sem.at[n], device_id=(seq_peer(1), ch), device_id_type=MESH,
        )
        whole.wait_recv()
        sent.append(whole)

    def gathered(send, recv, n):
        most = pl.ds(0, (seq_n - 1) * pack)
        whole = pltpu.make_async_remote_copy(
            src_ref=send.at[most], dst_ref=recv.at[most], send_sem=turn_send_sem.at[n],
            recv_sem=turn_recv_sem.at[n], device_id=(seq_peer(1), ch), device_id_type=MESH,
        )
        whole.wait_recv()
        sent.append(whole)

    def chunks_by_channel(turned, send):
        for q in range(quads):
            for c in range(OWNED):
                stage[pl.ds(q * OWNED + c, seq_n, pack), :] = turned[
                    c * seq_n : (c + 1) * seq_n, q * LANES : (q + 1) * LANES
                ]
        send[...] = stage[...].astype(BF16)

    def whole_document(recv):
        stage[...] = recv[...].astype(F32)
        return side_by_side([stage[pl.ds(c, blocks, OWNED), :] for c in range(OWNED)]).astype(BF16)

    loads[0].wait()
    chunks_by_channel(filt_vm[...].T, filt_send)
    pl.semaphore_wait(barrier, len(greeted))
    loads[2].wait()

    def ring_copy(held, left, right, sems, rows, kind):
        (lane_of, send_sem, recv_sem) = sems
        half = rows // 2
        own, spot, top, device = {
            "right_low": (1, 1, 0, right), "right_high": (1, 1, 1, right),
            "left_high": (1, 1, 1, left), "left_low": (1, 1, 0, left),
            "right_on": (0, 0, 0, right), "left_on": (0, 2, 1, left),
        }[kind]
        block = held(spot).at[pl.ds(top * half, half)]
        n = RING.index(kind)
        return pltpu.make_async_remote_copy(
            src_ref=block, dst_ref=block, send_sem=send_sem.at[(*lane_of, n)], recv_sem=recv_sem.at[(*lane_of, n)],
            device_id=device, device_id_type=MESH,
        )

    def feature_copy(kind):
        return ring_copy(
            lambda spot: feat.at[lax.rem(ch + ch_n - 1 + spot, ch_n)], (me, ch_peer(ch_n - 1)), (me, ch_peer(1)),
            ((), feat_send_sem, feat_recv_sem), rows_dev, kind,
        )

    ring_first = RING[:4] if ch_n == 4 else RING[:2]
    for kind in ring_first:
        go(feature_copy(kind))

    if z_n == 8:
        tell(0, [(seq_of(0, 2), ch), (seq_of(0, 6), ch)])
    loads[1].wait()
    for b in range(3):
        w_turned[b] = w_vm[b].T
    if z_n == 8:
        pl.semaphore_wait(heard_sem.at[0], 2)
    tell(1, [(seq_of(y, 0), ch) for y in range(1, y_n)])
    pages = lengths.shape[1]
    length_row = lengths[...].astype(F32)
    owner_row = owners[...].astype(F32)
    length_col = jnp.broadcast_to(length_row, (LANES, pages)).T
    owner_col = side_by_side([jnp.broadcast_to(owner_row, (LANES, pages)).T] * (pages // LANES))
    here = lax.broadcasted_iota(jnp.int32, (pages, pages), 0)
    other = lax.broadcasted_iota(jnp.int32, (pages, pages), 1)
    earlier = jnp.where(other < here, 1.0, 0.0)
    ahead = jnp.where(owner_row < owner_col, 1.0, jnp.where(owner_row == owner_col, earlier, 0.0))
    length_b = length_col.astype(BF16)
    placed = dot(ahead.astype(BF16), length_b)
    move = dot(earlier.astype(BF16), length_b) - placed
    move_high = jnp.floor(move * (1.0 / 256.0))
    move_low = move - 256.0 * move_high
    begin = side_by_side([placed] * quads)
    end = side_by_side([placed + length_col] * quads)
    position = (lax.broadcasted_iota(jnp.int32, (pages, rows_dev), 1) + me * rows_dev).astype(F32)
    inside = jnp.where(position >= begin, jnp.where(position < end, 1.0, 0.0), 0.0).astype(BF16)
    source = (
        position[:16]
        + 256.0 * dot(move_high.T[:16].astype(BF16), inside)
        + dot(move_low.T[:16].astype(BF16), inside)
    )
    source_block = jnp.floor(source * (1.0 / LANES))
    source_lane = source - LANES * source_block
    for q in range(quads):
        lanes = slice(q * LANES, (q + 1) * LANES)
        map_send[q : q + 1, :] = source_block[:1, lanes]
        map_send[quads + q : quads + q + 1, :] = source_lane[:1, lanes]
    if y_n > 1:
        pl.semaphore_wait(heard_sem.at[1], y_n - 1)
    tell(2, [(partner, ch)])
    pl.semaphore_wait(heard_sem.at[2], 1)

    scatter(filt_send, filt_recv, 0)
    map_recv[place] = map_send[...]
    same_core(lambda peer: map_send, lambda: map_recv.at[place], 3)
    if ch_n == 4:
        feature_copy("right_low").wait_recv()
        go(feature_copy("right_on"))
        feature_copy("left_high").wait_recv()
        go(feature_copy("left_on"))
    loads[6].wait()
    loads[7].wait()
    emb_turned = w_emb_vm[...].astype(F32).T.astype(BF16)
    term = dot(emb_turned, w_out_vm[...], ((1,), (1,)))
    for c in range(ch_n):
        term_send[c] = term[:, c * chan_dev : (c + 1) * chan_dev]

    def add_projection(source, first_time):
        block = feat[source]
        for b in range(3):
            lanes = pl.ds(pl.multiple_of(source * chan_dev, chan_dev), chan_dev)
            product = dot(w_turned[b, :, lanes], block, ((1,), (1,)))
            target = (gate_t, signal_t, spectrum)[b]
            if b == 2:
                view = pl.ds(0, chan_dev)
                for q in range(2):
                    lanes2 = slice(q * 2 * LANES, (q + 1) * 2 * LANES)
                    rows = pl.ds(q * chan_dev, chan_dev)
                    if first_time:
                        spectrum[rows, :] = product[:, lanes2]
                    else:
                        spectrum[rows, :] += product[:, lanes2]
            elif first_time:
                target[...] = product
            else:
                target[...] += product

    add_projection(ch, True)
    if ch_n == 4:
        feature_copy("right_high").wait_recv()
        add_projection(ch_peer(3), False)
        feature_copy("left_low").wait_recv()
        add_projection(ch_peer(1), False)
        feature_copy("right_on").wait_recv()
        feature_copy("left_on").wait_recv()
        add_projection(ch_peer(2), False)
    elif ch_n == 2:
        for kind in ring_first:
            feature_copy(kind).wait_recv()
        add_projection(ch_peer(1), False)
    value = side_by_side([spectrum[:chan_dev, :], spectrum[chan_dev : 2 * chan_dev, :]])
    signal_t[...] = signal_t[...] * value
    chunks_by_channel(signal_t[...], sig_send)
    scatter(sig_send, sig_recv, 1)

    def term_copy(i):
        return pltpu.make_async_remote_copy(
            src_ref=term_send.at[ch_peer(i)], dst_ref=term_recv.at[ch], send_sem=term_send_sem.at[i],
            recv_sem=term_recv_sem.at[i], device_id=(me, ch_peer(i)), device_id_type=MESH,
        )

    for i in range(1, ch_n):
        go(term_copy(i))
    term_recv[ch] = term_send[ch]

    gathered(filt_send, filt_recv, 0)
    for n in (3, 4, 5):
        loads[n].wait()
    spectrum[...] = forward(whole_document(filt_recv), first_v, twist_v, second_v)

    gathered(sig_send, sig_recv, 1)
    product = multiply(forward(whole_document(sig_recv), first_v, twist_v, second_v), spectrum[...])
    for n in (8, 9):
        loads[n].wait()
    convolved = backward(product, last_v, twist_v, second_back_v)
    for c in range(OWNED):
        stage[pl.ds(c, blocks, OWNED), :] = convolved[:, c * LANES : (c + 1) * LANES]
    conv_send[...] = stage[...].astype(BF16)
    scatter(conv_send, conv_recv, 2)

    for i in range(1, ch_n):
        term_copy(i).wait_recv()
    weight = term_recv[0]
    for c in range(1, ch_n):
        weight = weight + term_recv[c]
    weight_high[...], weight_low[...] = split(weight)
    all_in(map_recv, places - 1, 3)
    block_row = lax.broadcasted_iota(jnp.int32, (blocks, rows_dev), 0).astype(F32)

    @pl.loop(0, places)
    def _(d):
        row = side_by_side([map_recv[d, q : q + 1, :] for q in range(quads)])
        chosen[d] = jnp.where(block_row == row, 1.0, 0.0).astype(BF16)

    own_part = dot(emb_turned, feat[ch], ((1,), (1,)))
    bias_col = side_by_side([jnp.broadcast_to(bias[...], (LANES, chan_dev)).T] * quads)
    skipped = bias_col * signal_t[...]

    gathered(conv_send, conv_recv, 2)
    stage[...] = conv_recv[...].astype(F32)
    convolved_t = jnp.concatenate(
        [
            side_by_side([stage[pl.ds(q * OWNED + c, seq_n, pack), :] for q in range(quads)])
            for c in range(OWNED)
        ],
        axis=0,
    )
    mixed = ((convolved_t + skipped) * gate_t[...]).astype(BF16)
    embedded = (dot(weight_high[...], mixed) + dot(weight_low[...], mixed) + own_part)
    for c in range(ch_n):
        emb_send[c] = embedded[c * share : (c + 1) * share]

    def emb_copy(i):
        return pltpu.make_async_remote_copy(
            src_ref=emb_send.at[ch_peer(i)], dst_ref=emb_recv.at[ch], send_sem=emb_send_sem.at[i],
            recv_sem=emb_recv_sem.at[i], device_id=(me, ch_peer(i)), device_id_type=MESH,
        )

    for i in range(1, ch_n):
        go(emb_copy(i))
    emb_recv[ch] = emb_send[ch]
    for i in range(1, ch_n):
        emb_copy(i).wait_recv()
    total = emb_recv[0]
    for c in range(1, ch_n):
        total = total + emb_recv[c]
    def spread(rows, target):
        for q in range(quads):
            stage[pl.ds(q, places, quads), :] = rows[:, q * LANES : (q + 1) * LANES]
        target[...] = stage[: places * quads, :].astype(BF16).reshape(places, quads, LANES)

    spread(total, col_send)

    @pl.loop(1, seq_n)
    def _(i):
        peer = seq_peer(i)
        pltpu.make_async_remote_copy(
            src_ref=col_send.at[lax.div(peer, CORES)], dst_ref=col_recv.at[me], send_sem=turn_send_sem.at[4],
            recv_sem=turn_recv_sem.at[4], device_id=(peer, ch), device_id_type=MESH,
        ).start()

    col_recv[me] = col_send[place]
    all_in(col_recv, seq_n - 1, 4)
    column_t = col_recv[...].reshape(blocks, LANES).astype(F32).T.astype(BF16)
    lane_row = lax.broadcasted_iota(jnp.int32, (LANES, rows_dev), 0).astype(F32)

    def order_rows(d):
        found = dot(column_t, chosen[d])
        row = side_by_side([map_recv[d, quads + q : quads + q + 1, :] for q in range(quads)])
        picked = jnp.sum(jnp.where(lane_row == row, found, 0.0), axis=0, keepdims=True)
        lanes = [picked[:, q * LANES : (q + 1) * LANES] for q in range(quads)]
        out_send[d] = jnp.concatenate(lanes, axis=0).astype(BF16)

    def send_rows(d, first):
        for i in range(first, ch_n):
            pltpu.make_async_remote_copy(
                src_ref=out_send.at[d], dst_ref=out_recv.at[ch * places + place], send_sem=turn_send_sem.at[5],
                recv_sem=turn_recv_sem.at[5], device_id=(d * CORES + core, ch_peer(i)), device_id_type=MESH,
            ).start()

    @pl.loop(1, places)
    def _(i):
        d = lax.rem(place + i, places)
        order_rows(d)
        send_rows(d, 0)

    order_rows(place)
    send_rows(place, 1)
    out_recv[ch * places + place] = out_send[place]
    all_in(out_recv, ch_n * places - 1, 5)
    rows = ch_n * places
    stage[: rows * quads, :] = out_recv[...].reshape(rows * quads, LANES).astype(F32)
    out[...] = side_by_side([stage[pl.ds(q, rows, quads), :] for q in range(quads)]).T.astype(BF16)

    for copy in sent:
        copy.wait_send()


def body(sizes, features, w_in, bias_skip, filters, w_out, w_emb, page_lengths, page_owner):
    seq_n, ch_n, _, _ = sizes
    rows_dev, chan_dev = features.shape
    width, emb = w_out.shape[0], w_emb.shape[1]
    quads = rows_dev // LANES
    blocks = seq_n * quads
    turn_rows = seq_n * quads * OWNED
    places = seq_n // CORES
    share = emb // ch_n
    tables = [jnp.asarray(t) for t in transform_tables(blocks)]
    vmem, sem = pltpu.VMEM, pltpu.SemaphoreType.DMA
    turn = vmem((turn_rows, LANES), BF16)
    scratch = [
        vmem((ch_n, rows_dev, chan_dev), BF16),
        vmem((3, width, chan_dev), BF16),
        vmem((3, chan_dev, width), BF16),
        vmem((rows_dev, chan_dev), F32),
        vmem(w_out.shape, BF16),
        vmem(w_emb.shape, BF16),
        *(vmem(t.shape, t.dtype) for t in tables),
        vmem((turn_rows, LANES), F32),
        *([turn] * 6),
        vmem((chan_dev, rows_dev), F32),
        vmem((chan_dev, rows_dev), F32),
        vmem((OWNED * blocks, 2 * LANES), F32),
        vmem((ch_n, emb, chan_dev), F32),
        vmem((ch_n, emb, chan_dev), F32),
        vmem((emb, chan_dev), BF16),
        vmem((emb, chan_dev), BF16),
        vmem((ch_n, share, rows_dev), F32),
        vmem((ch_n, share, rows_dev), F32),
        vmem((2 * quads, LANES), F32),
        vmem((places, 2 * quads, LANES), F32),
        vmem((places, blocks, rows_dev), BF16),
        vmem((places, quads, LANES), BF16),
        vmem((seq_n, quads, LANES), BF16),
        vmem((places, quads, LANES), BF16),
        vmem((ch_n * places, quads, LANES), BF16),
        sem((10,)),
        sem((6,)), sem((6,)),
        sem((6,)), sem((6,)),
        sem((ch_n,)), sem((ch_n,)),
        sem((ch_n,)), sem((ch_n,)),
        pltpu.SemaphoreType.REGULAR((3,)),
    ]
    anywhere = pl.BlockSpec(memory_space=pl.ANY)
    inside = pl.BlockSpec(memory_space=pltpu.VMEM)
    return pl.pallas_call(
        functools.partial(layer_kernel, sizes),
        out_shape=jax.ShapeDtypeStruct((rows_dev, emb), BF16),
        in_specs=[anywhere, anywhere, inside, anywhere, anywhere, anywhere, inside, inside] + [anywhere] * 5,
        out_specs=inside,
        scratch_shapes=scratch,
        compiler_params=pltpu.CompilerParams(
            collective_id=0, has_side_effects=True, vmem_limit_bytes=60 * 1024 * 1024
        ),
        name="hyena_layer",
    )(
        features,
        jnp.transpose(w_in, (1, 0, 2)),
        bias_skip[None, :],
        filters,
        w_out,
        w_emb,
        page_lengths[None, :],
        page_owner[None, :],
        *tables,
    )


def solution(mesh, z_n=8):
    seq_n, ch_n = mesh.shape["seq"], mesh.shape["ch"]
    sizes = (seq_n, ch_n, seq_n // CORES // z_n, z_n)
    return jax.shard_map(
        functools.partial(body, sizes),
        mesh=mesh,
        in_specs=(
            P("seq", "ch"),
            P(None, None, "ch"),
            P("ch"),
            P("seq", "ch"),
            P(None, "ch"),
            P("ch", None),
            P(),
            P(),
        ),
        out_specs=P("seq", None),
        check_vma=False,
    )
```
